32 devices in a mesh: pp: 4 (over y, x), cp: 2 (over core), tp: 4 (over z).
Axes of the slice: x: 2, y: 2, z: 4, core: 2. Of those that a mesh axis runs over, the one named last changes fastest.
Arguments:
- query: bfloat16 [4, 384, 8192], P('pp', 'cp', 'tp'), may hold values from -125 to 125
- keys: bfloat16 [4, 384, 512], P('pp', 'cp', 'tp'), may hold values from -5 to 5
- values: bfloat16 [4, 384, 512], P('pp', 'cp', 'tp'), may hold values from -6 to 6
- attn_out: bfloat16 [4, 384, 8192], P('pp', 'cp', 'tp'), may hold values from -6 to 6
- grad_out: bfloat16 [4, 384, 8192], P('pp', 'cp', 'tp'), may hold values from -192 to 192
- span_pairs: int32 [2, 2], replicated, may hold values from 0 to 3, as said below
Outputs:
- key_grad: bfloat16 [4, 384, 512], P('pp', 'cp', 'tp')
- value_grad: bfloat16 [4, 384, 512], P('pp', 'cp', 'tp')
- upstream_grad: bfloat16 [4, 384, 8192], P('pp', 'cp', 'tp')
The draws below stay inside these ranges and needn't reach their ends.
Inputs may be any that keep to these rules, and one draw needn't show every extreme that they name: `span_pairs`: row r names the two spans of 96 positions held by context rank r, in either order; every span is named once.
All inputs are finite; a program needn't handle non-finite values.
Results may differ from the reference program's by a relative error of at most 0.0052.
Values may be sent and summed in bfloat16 or wider, within the bound.
A program may use at most 64 MiB of HBM per device.

```python
import math
import jax
import jax.numpy as jnp
from jax import lax

HEAD_DIM = 128
GROUP = 16
TOK_DEV = 192
SPAN = 96
TOKENS = 384
SPANS = 4
SECTIONS = 4
KV_HEADS = 4
Q_HEADS = 64


def draw_both(key):
    base = jax.random.fold_in(key, 4242)
    first, second = jax.random.split(base, 2)
    query_all = jnp.clip(jax.random.normal(first, (SECTIONS, TOKENS, Q_HEADS, HEAD_DIM), jnp.float32), -5.0, 5.0)
    key_all = jnp.clip(jax.random.normal(second, (SECTIONS, TOKENS, KV_HEADS, HEAD_DIM), jnp.float32), -5.0, 5.0)
    return (query_all, key_all)


def draw_query(key, part):
    query_all, key_all = draw_both(key)
    return query_all.reshape(SECTIONS, TOKENS, Q_HEADS * HEAD_DIM).astype(jnp.bfloat16)


def draw_keys(key, part):
    query_all, key_all = draw_both(key)
    return key_all.reshape(SECTIONS, TOKENS, KV_HEADS * HEAD_DIM).astype(jnp.bfloat16)


def draw_span_pairs(key, part):
    order = jax.random.permutation(jax.random.fold_in(key, 99), SPANS).astype(jnp.int32)
    return order.reshape(SPANS // 2, 2).astype(jnp.int32)


def steps_of(stream_key, shape, cuts, least, largest):
    factor_of, own = 1.0, jax.random.fold_in(stream_key, 6)
    for dim, shards_of in cuts:
        steps = jnp.exp(jax.random.uniform(jax.random.fold_in(own, dim), (shards_of,), jnp.float32, least / len(cuts), largest / len(cuts)))
        factor_of = factor_of * jnp.repeat(steps, shape[dim] // shards_of).reshape([-1 if axis == dim else 1 for axis in range(len(shape))])
    return factor_of


def scatter_about(own_key, extent, scale, reach, pieces=(), kind=jnp.bfloat16):
    gain = steps_of(own_key, extent, pieces, -0.22, 0.18) if pieces else 1.0
    entries = jax.random.normal(own_key, extent, jnp.float32) * scale * gain
    return jnp.minimum(jnp.maximum(entries, -reach), reach).astype(kind)


def setup_inputs(seed: int = 0) -> dict:
    splits = jax.random.split(jax.random.key(seed), 7)
    query = draw_query(jax.random.fold_in(splits[6], 71), 0)
    keys = draw_keys(jax.random.fold_in(splits[6], 71), 0)
    values = scatter_about(splits[2], (SECTIONS, TOKENS, KV_HEADS * HEAD_DIM), 1.0, 6.0, ((0, 4), (1, 2), (2, 4)))
    attn_out = scatter_about(splits[3], (SECTIONS, TOKENS, Q_HEADS * HEAD_DIM), 1.0, 6.0, ((0, 4), (1, 2), (2, 4)))
    grad_out = scatter_about(splits[4], (SECTIONS, TOKENS, Q_HEADS * HEAD_DIM), 32.0, 192.0, ((0, 4), (1, 2), (2, 4)))
    span_pairs = draw_span_pairs(jax.random.fold_in(splits[6], 71), 0)
    return {"query": query, "keys": keys, "values": values, "attn_out": attn_out, "grad_out": grad_out, "span_pairs": span_pairs}


def positions_of(span_pairs, tok_dev, span_len):
    row_ids = jnp.arange(span_pairs.shape[0] * tok_dev, dtype=jnp.int32)
    owners = row_ids // tok_dev
    halves = row_ids % tok_dev // span_len
    return (span_pairs[owners, halves] * span_len + row_ids % span_len).astype(jnp.int32)

def group_backward(query_group, key_rows, value_rows, output_group, grad_group, position):
    scale_factor = 1.0 / math.sqrt(HEAD_DIM)
    block_rows = min(512, TOKENS)
    block_count = TOKENS // block_rows

    def one_block(carry, block_index):
        start = block_index * block_rows
        query_block = lax.dynamic_slice_in_dim(query_group, start, block_rows, 0)
        grad_block = lax.dynamic_slice_in_dim(grad_group, start, block_rows, 0)
        output_block = lax.dynamic_slice_in_dim(output_group, start, block_rows, 0)
        query_pos = lax.dynamic_slice_in_dim(position, start, block_rows, 0)
        kept = (position[None, :] <= query_pos[:, None])[None]
        score = jnp.einsum('qhd,kd->hqk', query_block, key_rows) * scale_factor
        masked = jnp.where(kept, score, -jnp.inf)
        row_top = lax.optimization_barrier(jnp.max(masked, axis=-1, keepdims=True))
        log_mass = row_top + jnp.log(lax.optimization_barrier(jnp.sum(jnp.exp(masked - row_top), axis=-1, keepdims=True)))
        prob = jnp.exp(masked - log_mass)
        prob_low = lax.optimization_barrier(prob.astype(jnp.bfloat16)).astype(jnp.float32)
        dprob = jnp.einsum('qhd,kd->hqk', grad_block, value_rows)
        delta = jnp.einsum('qhd,qhd->hq', grad_block, output_block)
        dscore = prob * (dprob - delta[:, :, None]) * scale_factor
        dscore = lax.optimization_barrier(dscore.astype(jnp.bfloat16)).astype(jnp.float32)
        query_term = jnp.einsum('hqk,kd->qhd', dscore, key_rows)
        key_term = jnp.einsum('hqk,qhd->kd', dscore, query_block)
        value_term = jnp.einsum('hqk,qhd->kd', prob_low, grad_block)
        return ((carry[0] + key_term, carry[1] + value_term), query_term)
    zeros_init = jnp.zeros((TOKENS, HEAD_DIM), jnp.float32)
    (key_grad, value_grad), query_blocks = lax.scan(one_block, (zeros_init, zeros_init), jnp.arange(block_count, dtype=jnp.int32))
    return (query_blocks.reshape(TOKENS, GROUP * HEAD_DIM), key_grad, value_grad)

def reference(query, keys, values, attn_out, grad_out, span_pairs):
    position = positions_of(span_pairs, TOK_DEV, SPAN)
    width_q = GROUP * HEAD_DIM
    upstream_rows = []
    key_sections = []
    value_sections = []
    for section in range(SECTIONS):
        query_heads = []
        key_heads = []
        value_heads = []
        for group_id in range(KV_HEADS):
            key_rows = keys[section, :, group_id * HEAD_DIM:(group_id + 1) * HEAD_DIM].astype(jnp.float32)
            value_rows = values[section, :, group_id * HEAD_DIM:(group_id + 1) * HEAD_DIM].astype(jnp.float32)
            query_group = query[section, :, group_id * width_q:(group_id + 1) * width_q].astype(jnp.float32).reshape(TOKENS, GROUP, HEAD_DIM)
            output_group = attn_out[section, :, group_id * width_q:(group_id + 1) * width_q].astype(jnp.float32).reshape(TOKENS, GROUP, HEAD_DIM)
            grad_group = grad_out[section, :, group_id * width_q:(group_id + 1) * width_q].astype(jnp.float32).reshape(TOKENS, GROUP, HEAD_DIM)
            query_grad, key_grad, value_grad = group_backward(query_group, key_rows, value_rows, output_group, grad_group, position)
            query_heads.append(query_grad)
            key_heads.append(key_grad)
            value_heads.append(value_grad)
        upstream_rows.append(jnp.concatenate(query_heads, axis=1).astype(jnp.bfloat16))
        key_sections.append(jnp.concatenate(key_heads, axis=1).astype(jnp.bfloat16))
        value_sections.append(jnp.concatenate(value_heads, axis=1).astype(jnp.bfloat16))
    shifted = upstream_rows[1:] + [jnp.zeros_like(upstream_rows[0])]
    return (jnp.stack(key_sections), jnp.stack(value_sections), jnp.stack(shifted))
```

```python
import functools
import math

import jax
import jax.numpy as jnp
from jax import lax
from jax.experimental import pallas as pl
from jax.experimental.pallas import tpu as pltpu
from jax.sharding import PartitionSpec as P

MESH = pl.DeviceIdType.MESH
NEG = -1e30
LOG2E = math.log2(math.e)


def kernel(
    ranks, sections, block_len,
    pairs, query, keys, values, attn_out, grad_out,
    key_grad, value_grad, upstream,
    q_buf, o_buf, g_buf, k_buf, v_buf, dq_buf, bias, stats, dq_acc, pair_acc, pair_recv,
    in_sem, kv_send, kv_recv, dq_send, dq_recv, pair_send, pair_got,
):
    rows, width = q_buf.shape
    dim = k_buf.shape[1]
    heads = width // dim
    span = rows // 2
    seq = ranks * rows
    blocks = seq // block_len
    scale = 1.0 / math.sqrt(dim)
    me = lax.axis_index("cp")
    sec = lax.axis_index("pp")
    mine = pl.ds(pl.multiple_of(me * rows, rows), rows)

    own = [
        pltpu.make_async_copy(keys, k_buf.at[mine, :], in_sem.at[0]),
        pltpu.make_async_copy(values, v_buf.at[mine, :], in_sem.at[1]),
        pltpu.make_async_copy(query, q_buf, in_sem.at[2]),
        pltpu.make_async_copy(grad_out, g_buf, in_sem.at[3]),
        pltpu.make_async_copy(attn_out, o_buf, in_sem.at[4]),
    ]
    for copy in own:
        copy.start()

    barrier = pltpu.get_barrier_semaphore()
    for off in range(1, ranks):
        pl.semaphore_signal(
            barrier, inc=1, device_id={"cp": lax.rem(me + off, ranks)}, device_id_type=MESH
        )

    @pl.when(sec > 0)
    def _():
        pl.semaphore_signal(barrier, inc=1, device_id={"pp": sec - 1}, device_id_type=MESH)

    @pl.when(sec < sections - 1)
    def _():
        pl.semaphore_signal(barrier, inc=1, device_id={"pp": sec + 1}, device_id_type=MESH)

    row = lax.broadcasted_iota(jnp.int32, (rows, rows), 0)
    col = lax.broadcasted_iota(jnp.int32, (rows, rows), 1)
    q_pos = jnp.where(row < span, pairs[me, 0] * span, pairs[me, 1] * span - span) + row
    for r in range(ranks):
        k_pos = jnp.where(col < span, pairs[r, 0] * span, pairs[r, 1] * span - span) + col
        bias[:, r * rows:(r + 1) * rows] = jnp.where(k_pos <= q_pos, 0.0, NEG)
    pair_acc[...] = jnp.zeros_like(pair_acc)

    pl.semaphore_wait(
        barrier,
        ranks - 1 + (sec > 0).astype(jnp.int32) + (sec < sections - 1).astype(jnp.int32),
    )
    sent = []
    for off in range(1, ranks):
        for which, (src, buf) in enumerate(((keys, k_buf), (values, v_buf))):
            sent.append(
                pltpu.make_async_remote_copy(
                    src_ref=src,
                    dst_ref=buf.at[mine, :],
                    send_sem=kv_send.at[which, off - 1],
                    recv_sem=kv_recv.at[which, off - 1],
                    device_id={"cp": lax.rem(me + off, ranks)},
                    device_id_type=MESH,
                )
            )
    for copy in sent:
        copy.start()

    @pl.when(sec == sections - 1)
    def _():
        upstream[...] = jnp.zeros_like(upstream)

    for copy in own:
        copy.wait()
    for copy in sent:
        copy.wait_recv()

    def dot(a, b, da, db):
        return lax.dot_general(a, b, (((da,), (db,)), ((), ())), preferred_element_type=jnp.float32)

    def send_dq(h):
        lanes = pl.ds(pl.multiple_of(h * dim, dim), dim)
        return pltpu.make_async_remote_copy(
            src_ref=dq_buf.at[:, lanes],
            dst_ref=upstream.at[:, lanes],
            send_sem=dq_send.at[h],
            recv_sem=dq_recv.at[h],
            device_id={"pp": jnp.maximum(sec - 1, 0)},
            device_id_type=MESH,
        )

    def one_head(h, _):
        lanes = pl.ds(pl.multiple_of(h * dim, dim), dim)
        q = q_buf[:, lanes]
        g = g_buf[:, lanes]
        delta = jnp.sum(
            g.astype(jnp.float32) * o_buf[:, lanes].astype(jnp.float32), axis=1, keepdims=True
        )

        def scores(b):
            at = b * block_len if isinstance(b, int) else pl.multiple_of(b * block_len, block_len)
            part = pl.ds(at, block_len)
            return part, dot(q, k_buf[part, :], 1, 1) * (scale * LOG2E) + bias[:, part]

        def terms(part, prob):
            dprob = dot(g, v_buf[part, :], 1, 1)
            dscore = (prob * (dprob - delta) * scale).astype(jnp.bfloat16)
            return prob.astype(jnp.bfloat16), dscore, dot(dscore, k_buf[part, :], 1, 0)

        def pair_terms(part, prob_low, dscore):
            pair_acc[part, :dim] += dot(dscore, q, 0, 0)
            pair_acc[part, dim:] += dot(prob_low, g, 0, 0)

        def start_dq(dq):
            dq_buf[:, lanes] = dq.astype(jnp.bfloat16)

            @pl.when(sec > 0)
            def _():
                send_dq(h).start()

        if blocks == 1:
            part, score = scores(0)
            top = jnp.max(score, axis=1, keepdims=True)
            prob = jnp.exp2(score - top)
            prob = prob * (1.0 / jnp.sum(prob, axis=1, keepdims=True))
            prob_low, dscore, dq = terms(part, prob)
            start_dq(dq)
            pair_terms(part, prob_low, dscore)
        else:
            stats[0] = jnp.full((rows, 1), NEG, jnp.float32)
            stats[1] = jnp.zeros((rows, 1), jnp.float32)
            dq_acc[...] = jnp.zeros_like(dq_acc)

            def gather_stats(b, _):
                _, score = scores(b)
                before = stats[0]
                top = jnp.maximum(before, jnp.max(score, axis=1, keepdims=True))
                mass = jnp.sum(jnp.exp2(score - top), axis=1, keepdims=True)
                stats[1] = stats[1] * jnp.exp2(before - top) + mass
                stats[0] = top
                return 0

            def gather_terms(b, _):
                part, score = scores(b)
                prob = jnp.exp2(score - stats[0]) * (1.0 / stats[1])
                prob_low, dscore, dq = terms(part, prob)
                dq_acc[...] += dq
                pair_terms(part, prob_low, dscore)
                return 0

            lax.fori_loop(0, blocks, gather_stats, 0)
            lax.fori_loop(0, blocks, gather_terms, 0)
            start_dq(dq_acc[...])
        return 0

    lax.fori_loop(0, heads, one_head, 0)

    pair_sent = []
    for off in range(1, ranks):
        dst = lax.rem(me + off, ranks)
        pair_sent.append(
            pltpu.make_async_remote_copy(
                src_ref=pair_acc.at[pl.ds(pl.multiple_of(dst * rows, rows), rows), :],
                dst_ref=pair_recv.at[off - 1],
                send_sem=pair_send.at[off - 1],
                recv_sem=pair_got.at[off - 1],
                device_id={"cp": dst},
                device_id_type=MESH,
            )
        )
    for copy in pair_sent:
        copy.start()
    for copy in sent:
        copy.wait_send()
    for copy in pair_sent:
        copy.wait_recv()
    total = pair_acc[mine, :]
    for off in range(1, ranks):
        total = total + pair_recv[off - 1]
    key_grad[...] = total[:, :dim].astype(jnp.bfloat16)
    value_grad[...] = total[:, dim:].astype(jnp.bfloat16)
    for copy in pair_sent:
        copy.wait_send()

    @pl.when(sec > 0)
    def _():
        for h in range(heads):
            send_dq(h).wait_send()

    @pl.when(sec < sections - 1)
    def _():
        for h in range(heads):
            send_dq(h).wait_recv()


def body(query, keys, values, attn_out, grad_out, span_pairs):
    _, rows, width = query.shape
    dim = keys.shape[2]
    heads = width // dim
    ranks = lax.axis_size("cp")
    sections = lax.axis_size("pp")
    seq = ranks * rows
    block_len = 2 * rows if ranks % 2 == 0 else rows
    low, full = jnp.bfloat16, jnp.float32
    dma = pltpu.SemaphoreType.DMA
    others = max(ranks - 1, 1)
    vmem = pl.BlockSpec(memory_space=pltpu.VMEM)
    hbm = pl.BlockSpec(memory_space=pltpu.HBM)
    key_grad, value_grad, upstream = pl.pallas_call(
        functools.partial(kernel, ranks, sections, block_len),
        out_shape=(
            jax.ShapeDtypeStruct((rows, dim), low),
            jax.ShapeDtypeStruct((rows, dim), low),
            jax.ShapeDtypeStruct((rows, width), low),
        ),
        in_specs=[pl.BlockSpec(memory_space=pltpu.SMEM)] + [hbm] * 5,
        out_specs=(vmem, vmem, vmem),
        scratch_shapes=[
            pltpu.VMEM((rows, width), low),
            pltpu.VMEM((rows, width), low),
            pltpu.VMEM((rows, width), low),
            pltpu.VMEM((seq, dim), low),
            pltpu.VMEM((seq, dim), low),
            pltpu.VMEM((rows, width), low),
            pltpu.VMEM((rows, seq), full),
            pltpu.VMEM((2, rows, 1), full),
            pltpu.VMEM((rows, dim), full),
            pltpu.VMEM((seq, 2 * dim), full),
            pltpu.VMEM((others, rows, 2 * dim), full),
            dma((5,)),
            dma((2, others)),
            dma((2, others)),
            dma((heads,)),
            dma((heads,)),
            dma((others,)),
            dma((others,)),
        ],
        compiler_params=pltpu.CompilerParams(
            collective_id=0, has_side_effects=True, vmem_limit_bytes=48 * 1024 * 1024
        ),
        name="backward",
    )(span_pairs, query[0], keys[0], values[0], attn_out[0], grad_out[0])
    return key_grad[None], value_grad[None], upstream[None]


def solution(mesh):
    spec = P("pp", "cp", "tp")
    return jax.shard_map(
        body,
        mesh=mesh,
        in_specs=(spec, spec, spec, spec, spec, P()),
        out_specs=(spec, spec, spec),
        check_vma=False,
    )
```

```python
import functools
import math

import jax
import jax.numpy as jnp
from jax import lax
from jax.experimental import pallas as pl
from jax.experimental.pallas import tpu as pltpu
from jax.sharding import PartitionSpec as P

MESH = pl.DeviceIdType.MESH
NEG = -1e30
LOG2E = math.log2(math.e)


def kernel(
    ranks, sections, block_len,
    pairs, query, keys, values, attn_out, grad_out,
    key_grad, value_grad, upstream,
    q_buf, o_buf, g_buf, k_buf, v_buf, dq_buf, bias, stats, dq_acc, pair_acc, pair_recv,
    in_sem, kv_send, kv_recv, dq_send, dq_recv, pair_send, pair_got,
):
    rows, width = q_buf.shape
    dim = k_buf.shape[1]
    heads = width // dim
    span = rows // 2
    seq = ranks * rows
    blocks = seq // block_len
    scale = 1.0 / math.sqrt(dim)
    me = lax.axis_index("cp")
    sec = lax.axis_index("pp")
    mine = pl.ds(pl.multiple_of(me * rows, rows), rows)

    own = [
        pltpu.make_async_copy(keys, k_buf.at[mine, :], in_sem.at[0]),
        pltpu.make_async_copy(values, v_buf.at[mine, :], in_sem.at[1]),
        pltpu.make_async_copy(query, q_buf, in_sem.at[2]),
        pltpu.make_async_copy(grad_out, g_buf, in_sem.at[3]),
        pltpu.make_async_copy(attn_out, o_buf, in_sem.at[4]),
    ]
    for copy in own:
        copy.start()

    barrier = pltpu.get_barrier_semaphore()
    for off in range(1, ranks):
        pl.semaphore_signal(
            barrier, inc=1, device_id={"cp": lax.rem(me + off, ranks)}, device_id_type=MESH
        )

    @pl.when(sec > 0)
    def _():
        pl.semaphore_signal(barrier, inc=1, device_id={"pp": sec - 1}, device_id_type=MESH)

    @pl.when(sec < sections - 1)
    def _():
        pl.semaphore_signal(barrier, inc=1, device_id={"pp": sec + 1}, device_id_type=MESH)

    row = lax.broadcasted_iota(jnp.int32, (rows, rows), 0)
    col = lax.broadcasted_iota(jnp.int32, (rows, rows), 1)
    q_pos = jnp.where(row < span, pairs[me, 0] * span, pairs[me, 1] * span - span) + row
    for r in range(ranks):
        k_pos = jnp.where(col < span, pairs[r, 0] * span, pairs[r, 1] * span - span) + col
        bias[:, r * rows:(r + 1) * rows] = jnp.where(k_pos <= q_pos, 0.0, NEG)
    pair_acc[...] = jnp.zeros_like(pair_acc)

    pl.semaphore_wait(
        barrier,
        ranks - 1 + (sec > 0).astype(jnp.int32) + (sec < sections - 1).astype(jnp.int32),
    )
    sent = []
    for off in range(1, ranks):
        for which, (src, buf) in enumerate(((keys, k_buf), (values, v_buf))):
            sent.append(
                pltpu.make_async_remote_copy(
                    src_ref=src,
                    dst_ref=buf.at[mine, :],
                    send_sem=kv_send.at[which, off - 1],
                    recv_sem=kv_recv.at[which, off - 1],
                    device_id={"cp": lax.rem(me + off, ranks)},
                    device_id_type=MESH,
                )
            )
    for copy in sent:
        copy.start()

    @pl.when(sec == sections - 1)
    def _():
        upstream[...] = jnp.zeros_like(upstream)

    for copy in own:
        copy.wait()
    for copy in sent:
        copy.wait_recv()

    def dot(a, b, da, db):
        return lax.dot_general(a, b, (((da,), (db,)), ((), ())), preferred_element_type=jnp.float32)

    def send_dq(h):
        lanes = pl.ds(pl.multiple_of(h * dim, dim), dim)
        return pltpu.make_async_remote_copy(
            src_ref=dq_buf.at[:, lanes],
            dst_ref=upstream.at[:, lanes],
            send_sem=dq_send.at[h],
            recv_sem=dq_recv.at[h],
            device_id={"pp": jnp.maximum(sec - 1, 0)},
            device_id_type=MESH,
        )

    def one_head(h, _):
        lanes = pl.ds(pl.multiple_of(h * dim, dim), dim)
        q = q_buf[:, lanes]
        g = g_buf[:, lanes]
        delta = jnp.sum(
            g.astype(jnp.float32) * o_buf[:, lanes].astype(jnp.float32), axis=1, keepdims=True
        )

        def scores(b):
            at = b * block_len if isinstance(b, int) else pl.multiple_of(b * block_len, block_len)
            part = pl.ds(at, block_len)
            return part, dot(q, k_buf[part, :], 1, 1) * (scale * LOG2E) + bias[:, part]

        def terms(part, prob):
            dprob = dot(g, v_buf[part, :], 1, 1)
            dscore = (prob * (dprob - delta) * scale).astype(jnp.bfloat16)
            return prob.astype(jnp.bfloat16), dscore, dot(dscore, k_buf[part, :], 1, 0)

        def pair_terms(part, prob_low, dscore):
            pair_acc[part, :dim] += dot(dscore, q, 0, 0)
            pair_acc[part, dim:] += dot(prob_low, g, 0, 0)

        def start_dq(dq):
            dq_buf[:, lanes] = dq.astype(jnp.bfloat16)

            @pl.when(sec > 0)
            def _():
                send_dq(h).start()

        if blocks == 1:
            part, score = scores(0)
            top = jnp.max(score, axis=1, keepdims=True)
            prob = jnp.exp2(score - top)
            prob = prob * (1.0 / jnp.sum(prob, axis=1, keepdims=True))
            prob_low, dscore, dq = terms(part, prob)
            start_dq(dq)
            pair_terms(part, prob_low, dscore)
        else:
            stats[0] = jnp.full((rows, 1), NEG, jnp.float32)
            stats[1] = jnp.zeros((rows, 1), jnp.float32)
            dq_acc[...] = jnp.zeros_like(dq_acc)

            def gather_stats(b, _):
                _, score = scores(b)
                before = stats[0]
                top = jnp.maximum(before, jnp.max(score, axis=1, keepdims=True))
                mass = jnp.sum(jnp.exp2(score - top), axis=1, keepdims=True)
                stats[1] = stats[1] * jnp.exp2(before - top) + mass
                stats[0] = top
                return 0

            def gather_terms(b, _):
                part, score = scores(b)
                prob = jnp.exp2(score - stats[0]) * (1.0 / stats[1])
                prob_low, dscore, dq = terms(part, prob)
                dq_acc[...] += dq
                pair_terms(part, prob_low, dscore)
                return 0

            lax.fori_loop(0, blocks, gather_stats, 0)
            lax.fori_loop(0, blocks, gather_terms, 0)
            start_dq(dq_acc[...])
        return 0

    lax.fori_loop(0, heads, one_head, 0)

    pair_sent = []
    for off in range(1, ranks):
        dst = lax.rem(me + off, ranks)
        pair_sent.append(
            pltpu.make_async_remote_copy(
                src_ref=pair_acc.at[pl.ds(pl.multiple_of(dst * rows, rows), rows), :],
                dst_ref=pair_recv.at[off - 1],
                send_sem=pair_send.at[off - 1],
                recv_sem=pair_got.at[off - 1],
                device_id={"cp": dst},
                device_id_type=MESH,
            )
        )
    for copy in pair_sent:
        copy.start()
    for copy in sent:
        copy.wait_send()
    for copy in pair_sent:
        copy.wait_recv()
    total = pair_acc[mine, :]
    for off in range(1, ranks):
        total = total + pair_recv[off - 1]
    key_grad[...] = total[:, :dim].astype(jnp.bfloat16)
    value_grad[...] = total[:, dim:].astype(jnp.bfloat16)
    for copy in pair_sent:
        copy.wait_send()

    @pl.when(sec > 0)
    def _():
        for h in range(heads):
            send_dq(h).wait_send()

    @pl.when(sec < sections - 1)
    def _():
        for h in range(heads):
            send_dq(h).wait_recv()


def store(key_grad, value_grad, upstream, key_out, value_out, upstream_out, sem):
    copies = [
        pltpu.make_async_copy(src, dst, sem.at[i])
        for i, (src, dst) in enumerate(
            ((upstream, upstream_out), (key_grad, key_out), (value_grad, value_out))
        )
    ]
    for copy in copies:
        copy.start()
    for copy in copies:
        copy.wait()


def body(query, keys, values, attn_out, grad_out, span_pairs):
    _, rows, width = query.shape
    dim = keys.shape[2]
    heads = width // dim
    ranks = lax.axis_size("cp")
    sections = lax.axis_size("pp")
    seq = ranks * rows
    block_len = 2 * rows if ranks % 2 == 0 else rows
    low, full = jnp.bfloat16, jnp.float32
    dma = pltpu.SemaphoreType.DMA
    others = max(ranks - 1, 1)
    vmem = pl.BlockSpec(memory_space=pltpu.VMEM)
    hbm = pl.BlockSpec(memory_space=pltpu.HBM)
    key_grad, value_grad, upstream = pl.pallas_call(
        functools.partial(kernel, ranks, sections, block_len),
        out_shape=(
            pltpu.VMEM((rows, dim), low),
            pltpu.VMEM((rows, dim), low),
            pltpu.VMEM((rows, width), low),
        ),
        in_specs=[pl.BlockSpec(memory_space=pltpu.SMEM)] + [hbm] * 5,
        out_specs=(vmem, vmem, vmem),
        scratch_shapes=[
            pltpu.VMEM((rows, width), low),
            pltpu.VMEM((rows, width), low),
            pltpu.VMEM((rows, width), low),
            pltpu.VMEM((seq, dim), low),
            pltpu.VMEM((seq, dim), low),
            pltpu.VMEM((rows, width), low),
            pltpu.VMEM((rows, seq), full),
            pltpu.VMEM((2, rows, 1), full),
            pltpu.VMEM((rows, dim), full),
            pltpu.VMEM((seq, 2 * dim), full),
            pltpu.VMEM((others, rows, 2 * dim), full),
            dma((5,)),
            dma((2, others)),
            dma((2, others)),
            dma((heads,)),
            dma((heads,)),
            dma((others,)),
            dma((others,)),
        ],
        compiler_params=pltpu.CompilerParams(
            collective_id=0, has_side_effects=True, vmem_limit_bytes=64 * 1024 * 1024 - 1200 * 1024
        ),
        name="backward",
    )(span_pairs, query[0], keys[0], values[0], attn_out[0], grad_out[0])
    anywhere = pl.BlockSpec(memory_space=pl.ANY)
    key_grad, value_grad, upstream = pl.pallas_call(
        store,
        out_shape=(
            jax.ShapeDtypeStruct((rows, dim), low),
            jax.ShapeDtypeStruct((rows, dim), low),
            jax.ShapeDtypeStruct((rows, width), low),
        ),
        in_specs=[anywhere] * 3,
        out_specs=(anywhere,) * 3,
        scratch_shapes=[dma((3,))],
        compiler_params=pltpu.CompilerParams(vmem_limit_bytes=1024 * 1024),
        name="store",
    )(key_grad, value_grad, upstream)
    return key_grad[None], value_grad[None], upstream[None]


def solution(mesh):
    spec = P("pp", "cp", "tp")
    return jax.shard_map(
        body,
        mesh=mesh,
        in_specs=(spec, spec, spec, spec, spec, P()),
        out_specs=(spec, spec, spec),
        check_vma=False,
    )
```

```python
import functools
import math

import jax
import jax.numpy as jnp
from jax import lax
from jax.experimental import pallas as pl
from jax.experimental.pallas import tpu as pltpu
from jax.sharding import PartitionSpec as P

MESH = pl.DeviceIdType.MESH
NEG = -1e30
LOG2E = math.log2(math.e)


def gather(
    ranks,
    pairs, query, keys, values, attn_out, grad_out,
    q_buf, o_buf, g_buf, k_buf, v_buf, bias,
    in_sem, kv_send, kv_recv,
):
    rows = q_buf.shape[0]
    span = rows // 2
    me = lax.axis_index("cp")
    mine = pl.ds(pl.multiple_of(me * rows, rows), rows)

    barrier = pltpu.get_barrier_semaphore()
    for off in range(1, ranks):
        pl.semaphore_signal(
            barrier, inc=1, device_id={"cp": lax.rem(me + off, ranks)}, device_id_type=MESH
        )
    own = [
        pltpu.make_async_copy(keys, k_buf.at[mine, :], in_sem.at[0]),
        pltpu.make_async_copy(values, v_buf.at[mine, :], in_sem.at[1]),
        pltpu.make_async_copy(query, q_buf, in_sem.at[2]),
        pltpu.make_async_copy(grad_out, g_buf, in_sem.at[3]),
        pltpu.make_async_copy(attn_out, o_buf, in_sem.at[4]),
    ]
    for copy in own:
        copy.start()
    pl.semaphore_wait(barrier, ranks - 1)
    sent = []
    for off in range(1, ranks):
        for which, (src, buf) in enumerate(((keys, k_buf), (values, v_buf))):
            sent.append(
                pltpu.make_async_remote_copy(
                    src_ref=src,
                    dst_ref=buf.at[mine, :],
                    send_sem=kv_send.at[which, off - 1],
                    recv_sem=kv_recv.at[which, off - 1],
                    device_id={"cp": lax.rem(me + off, ranks)},
                    device_id_type=MESH,
                )
            )
    for copy in sent:
        copy.start()

    row = lax.broadcasted_iota(jnp.int32, (rows, rows), 0)
    col = lax.broadcasted_iota(jnp.int32, (rows, rows), 1)
    q_pos = jnp.where(row < span, pairs[me, 0] * span, pairs[me, 1] * span - span) + row
    for r in range(ranks):
        k_pos = jnp.where(col < span, pairs[r, 0] * span, pairs[r, 1] * span - span) + col
        bias[:, r * rows:(r + 1) * rows] = jnp.where(k_pos <= q_pos, 0.0, NEG)

    for copy in own:
        copy.wait()
    for copy in sent:
        copy.wait()


def kernel(
    ranks, sections, block_len,
    q_buf, o_buf, g_buf, k_buf, v_buf, bias,
    key_grad, value_grad, upstream,
    dq_buf, stats, dq_acc, pair_acc, pair_recv,
    dq_send, dq_recv, pair_send, pair_got,
):
    rows, width = q_buf.shape
    dim = k_buf.shape[1]
    heads = width // dim
    seq = ranks * rows
    blocks = seq // block_len
    scale = 1.0 / math.sqrt(dim)
    me = lax.axis_index("cp")
    sec = lax.axis_index("pp")
    mine = pl.ds(pl.multiple_of(me * rows, rows), rows)

    barrier = pltpu.get_barrier_semaphore()
    for off in range(1, ranks):
        pl.semaphore_signal(
            barrier, inc=1, device_id={"cp": lax.rem(me + off, ranks)}, device_id_type=MESH
        )

    @pl.when(sec > 0)
    def _():
        pl.semaphore_signal(barrier, inc=1, device_id={"pp": sec - 1}, device_id_type=MESH)

    @pl.when(sec < sections - 1)
    def _():
        pl.semaphore_signal(barrier, inc=1, device_id={"pp": sec + 1}, device_id_type=MESH)

    pair_acc[...] = jnp.zeros_like(pair_acc)

    def dot(a, b, da, db):
        return lax.dot_general(a, b, (((da,), (db,)), ((), ())), preferred_element_type=jnp.float32)

    def enter():
        pl.semaphore_wait(
            barrier,
            ranks - 1 + (sec > 0).astype(jnp.int32) + (sec < sections - 1).astype(jnp.int32),
        )

    def lanes_of(h):
        return pl.ds(h * dim if isinstance(h, int) else pl.multiple_of(h * dim, dim), dim)

    def send_dq(h):
        lanes = lanes_of(h)
        return pltpu.make_async_remote_copy(
            src_ref=dq_buf.at[:, lanes],
            dst_ref=upstream.at[:, lanes],
            send_sem=dq_send.at[h],
            recv_sem=dq_recv.at[h],
            device_id={"pp": jnp.maximum(sec - 1, 0)},
            device_id_type=MESH,
        )

    def one_head(h, _):
        lanes = lanes_of(h)
        q = q_buf[:, lanes]
        g = g_buf[:, lanes]
        delta = jnp.sum(
            g.astype(jnp.float32) * o_buf[:, lanes].astype(jnp.float32), axis=1, keepdims=True
        )

        def scores(b):
            at = b * block_len if isinstance(b, int) else pl.multiple_of(b * block_len, block_len)
            part = pl.ds(at, block_len)
            return part, dot(q, k_buf[part, :], 1, 1) * (scale * LOG2E) + bias[:, part]

        def terms(part, prob):
            dprob = dot(g, v_buf[part, :], 1, 1)
            dscore = (prob * (dprob - delta) * scale).astype(jnp.bfloat16)
            return prob.astype(jnp.bfloat16), dscore, dot(dscore, k_buf[part, :], 1, 0)

        def pair_terms(part, prob_low, dscore):
            pair_acc[part, :dim] += dot(dscore, q, 0, 0)
            pair_acc[part, dim:] += dot(prob_low, g, 0, 0)

        def start_dq(dq):
            dq_buf[:, lanes] = dq.astype(jnp.bfloat16)

            if isinstance(h, int):
                enter()

            @pl.when(sec > 0)
            def _():
                send_dq(h).start()

        if blocks == 1:
            part, score = scores(0)
            top = jnp.max(score, axis=1, keepdims=True)
            prob = jnp.exp2(score - top)
            prob = prob * (1.0 / jnp.sum(prob, axis=1, keepdims=True))
            prob_low, dscore, dq = terms(part, prob)
            start_dq(dq)
            pair_terms(part, prob_low, dscore)
        else:
            stats[0] = jnp.full((rows, 1), NEG, jnp.float32)
            stats[1] = jnp.zeros((rows, 1), jnp.float32)
            dq_acc[...] = jnp.zeros_like(dq_acc)

            def gather_stats(b, _):
                _, score = scores(b)
                before = stats[0]
                top = jnp.maximum(before, jnp.max(score, axis=1, keepdims=True))
                mass = jnp.sum(jnp.exp2(score - top), axis=1, keepdims=True)
                stats[1] = stats[1] * jnp.exp2(before - top) + mass
                stats[0] = top
                return 0

            def gather_terms(b, _):
                part, score = scores(b)
                prob = jnp.exp2(score - stats[0]) * (1.0 / stats[1])
                prob_low, dscore, dq = terms(part, prob)
                dq_acc[...] += dq
                pair_terms(part, prob_low, dscore)
                return 0

            lax.fori_loop(0, blocks, gather_stats, 0)
            lax.fori_loop(0, blocks, gather_terms, 0)
            start_dq(dq_acc[...])
        return 0

    one_head(0, 0)

    @pl.when(sec == sections - 1)
    def _():
        upstream[...] = jnp.zeros_like(upstream)

    lax.fori_loop(1, heads, one_head, 0)

    pair_sent = []
    for off in range(1, ranks):
        dst = lax.rem(me + off, ranks)
        pair_sent.append(
            pltpu.make_async_remote_copy(
                src_ref=pair_acc.at[pl.ds(pl.multiple_of(dst * rows, rows), rows), :],
                dst_ref=pair_recv.at[off - 1],
                send_sem=pair_send.at[off - 1],
                recv_sem=pair_got.at[off - 1],
                device_id={"cp": dst},
                device_id_type=MESH,
            )
        )
    for copy in pair_sent:
        copy.start()
    for copy in pair_sent:
        copy.wait_recv()
    total = pair_acc[mine, :]
    for off in range(1, ranks):
        total = total + pair_recv[off - 1]
    key_grad[...] = total[:, :dim].astype(jnp.bfloat16)
    value_grad[...] = total[:, dim:].astype(jnp.bfloat16)
    for copy in pair_sent:
        copy.wait_send()

    @pl.when(sec > 0)
    def _():
        for h in range(heads):
            send_dq(h).wait_send()

    @pl.when(sec < sections - 1)
    def _():
        for h in range(heads):
            send_dq(h).wait_recv()


def store(key_grad, value_grad, upstream, key_out, value_out, upstream_out, sem):
    copies = [
        pltpu.make_async_copy(src, dst, sem.at[i])
        for i, (src, dst) in enumerate(
            ((upstream, upstream_out), (key_grad, key_out), (value_grad, value_out))
        )
    ]
    for copy in copies:
        copy.start()
    for copy in copies:
        copy.wait()


def body(query, keys, values, attn_out, grad_out, span_pairs):
    _, rows, width = query.shape
    dim = keys.shape[2]
    heads = width // dim
    ranks = lax.axis_size("cp")
    sections = lax.axis_size("pp")
    seq = ranks * rows
    block_len = 2 * rows if ranks % 2 == 0 else rows
    low, full = jnp.bfloat16, jnp.float32
    dma = pltpu.SemaphoreType.DMA
    others = max(ranks - 1, 1)
    vmem = pl.BlockSpec(memory_space=pltpu.VMEM)
    hbm = pl.BlockSpec(memory_space=pltpu.HBM)
    gathered = (
        ((rows, width), low),
        ((rows, width), low),
        ((rows, width), low),
        ((seq, dim), low),
        ((seq, dim), low),
        ((rows, seq), full),
    )
    held = sum(math.prod(shape) * jnp.dtype(kind).itemsize for shape, kind in gathered)
    inputs = pl.pallas_call(
        functools.partial(gather, ranks),
        out_shape=tuple(pltpu.VMEM(shape, kind) for shape, kind in gathered),
        in_specs=[pl.BlockSpec(memory_space=pltpu.SMEM)] + [hbm] * 5,
        out_specs=(vmem,) * 6,
        scratch_shapes=[dma((5,)), dma((2, others)), dma((2, others))],
        compiler_params=pltpu.CompilerParams(
            collective_id=1,
            has_side_effects=True,
            vmem_limit_bytes=64 * 1024 * 1024 - held - 128 * 1024,
        ),
        name="gather",
    )(span_pairs, query[0], keys[0], values[0], attn_out[0], grad_out[0])
    key_grad, value_grad, upstream = pl.pallas_call(
        functools.partial(kernel, ranks, sections, block_len),
        out_shape=(
            pltpu.VMEM((rows, dim), low),
            pltpu.VMEM((rows, dim), low),
            pltpu.VMEM((rows, width), low),
        ),
        in_specs=[vmem] * 6,
        out_specs=(vmem, vmem, vmem),
        scratch_shapes=[
            pltpu.VMEM((rows, width), low),
            pltpu.VMEM((2, rows, 1), full),
            pltpu.VMEM((rows, dim), full),
            pltpu.VMEM((seq, 2 * dim), full),
            pltpu.VMEM((others, rows, 2 * dim), full),
            dma((heads,)),
            dma((heads,)),
            dma((others,)),
            dma((others,)),
        ],
        compiler_params=pltpu.CompilerParams(
            collective_id=0, has_side_effects=True, vmem_limit_bytes=32 * 1024 * 1024
        ),
        name="backward",
    )(*inputs)
    anywhere = pl.BlockSpec(memory_space=pl.ANY)
    key_grad, value_grad, upstream = pl.pallas_call(
        store,
        out_shape=(
            jax.ShapeDtypeStruct((rows, dim), low),
            jax.ShapeDtypeStruct((rows, dim), low),
            jax.ShapeDtypeStruct((rows, width), low),
        ),
        in_specs=[anywhere] * 3,
        out_specs=(anywhere,) * 3,
        scratch_shapes=[dma((3,))],
        compiler_params=pltpu.CompilerParams(vmem_limit_bytes=1024 * 1024),
        name="store",
    )(key_grad, value_grad, upstream)
    return key_grad[None], value_grad[None], upstream[None]


def solution(mesh):
    spec = P("pp", "cp", "tp")
    return jax.shard_map(
        body,
        mesh=mesh,
        in_specs=(spec, spec, spec, spec, spec, P()),
        out_specs=(spec, spec, spec),
        check_vma=False,
    )
```

```python
import functools
import math

import jax
import jax.numpy as jnp
from jax import lax
from jax.experimental import pallas as pl
from jax.experimental.pallas import tpu as pltpu
from jax.sharding import PartitionSpec as P

MESH = pl.DeviceIdType.MESH
NEG = -1e30
LOG2E = math.log2(math.e)


def kernel(
    ranks, sections, block_len,
    pairs, query, keys, values, attn_out, grad_out,
    key_grad, value_grad, upstream,
    q_buf, o_buf, g_buf, k_buf, v_buf, dq_buf, bias, stats, dq_acc, pair_acc, pair_recv,
    in_sem, kv_send, kv_recv, dq_send, dq_recv, pair_send, pair_got,
):
    rows, width = q_buf.shape
    dim = k_buf.shape[1]
    heads = width // dim
    span = rows // 2
    seq = ranks * rows
    blocks = seq // block_len
    scale = 1.0 / math.sqrt(dim)
    me = lax.axis_index("cp")
    sec = lax.axis_index("pp")
    mine = pl.ds(0, rows)

    barrier = pltpu.get_barrier_semaphore()
    for off in range(1, ranks):
        pl.semaphore_signal(
            barrier, inc=1, device_id={"cp": lax.rem(me + off, ranks)}, device_id_type=MESH
        )

    @pl.when(sec < sections - 1)
    def _():
        pl.semaphore_signal(barrier, inc=1, device_id={"pp": sec + 1}, device_id_type=MESH)

    own = [
        pltpu.make_async_copy(keys, k_buf.at[mine, :], in_sem.at[0]),
        pltpu.make_async_copy(values, v_buf.at[mine, :], in_sem.at[1]),
    ]
    first, rest = pl.ds(0, dim), pl.ds(dim, width - dim)
    wide = ((query, q_buf), (grad_out, g_buf), (attn_out, o_buf))
    begin = [
        pltpu.make_async_copy(src.at[:, first], dst.at[:, first], in_sem.at[2 + i])
        for i, (src, dst) in enumerate(wide)
    ]
    later = [
        pltpu.make_async_copy(src.at[:, rest], dst.at[:, rest], in_sem.at[5 + i])
        for i, (src, dst) in enumerate(wide)
    ]
    for copy in own + begin:
        copy.start()

    pl.semaphore_wait(barrier, ranks - 1 + (sec > 0).astype(jnp.int32))
    sent = []
    for off in range(1, ranks):
        for which, (src, buf) in enumerate(((keys, k_buf), (values, v_buf))):
            sent.append(
                pltpu.make_async_remote_copy(
                    src_ref=src,
                    dst_ref=buf.at[pl.ds((ranks - off) * rows, rows), :],
                    send_sem=kv_send.at[which, off - 1],
                    recv_sem=kv_recv.at[which, off - 1],
                    device_id={"cp": lax.rem(me + off, ranks)},
                    device_id_type=MESH,
                )
            )
    for copy in sent + later:
        copy.start()

    row = lax.broadcasted_iota(jnp.int32, (rows, rows), 0)
    col = lax.broadcasted_iota(jnp.int32, (rows, rows), 1)
    q_pos = jnp.where(row < span, pairs[me, 0] * span, pairs[me, 1] * span - span) + row
    for r in range(ranks):
        rank = lax.rem(me + r, ranks)
        k_pos = jnp.where(col < span, pairs[rank, 0] * span, pairs[rank, 1] * span - span) + col
        bias[:, r * rows:(r + 1) * rows] = jnp.where(k_pos <= q_pos, 0.0, NEG)
    pair_acc[...] = jnp.zeros_like(pair_acc)

    for copy in own + begin:
        copy.wait()
    for copy in sent:
        copy.wait_recv()

    def dot(a, b, da, db):
        return lax.dot_general(a, b, (((da,), (db,)), ((), ())), preferred_element_type=jnp.float32)

    def lanes_of(h):
        return pl.ds(h * dim if isinstance(h, int) else pl.multiple_of(h * dim, dim), dim)

    def send_dq(h, lines, slot):
        return pltpu.make_async_remote_copy(
            src_ref=dq_buf.at[lines, lanes_of(h)],
            dst_ref=upstream.at[lines, lanes_of(h)],
            send_sem=dq_send.at[slot],
            recv_sem=dq_recv.at[slot],
            device_id={"pp": jnp.maximum(sec - 1, 0)},
            device_id_type=MESH,
        )

    def rows_of_head(h, lines, slot):
        lanes = lanes_of(h)
        q = q_buf[lines, lanes]
        g = g_buf[lines, lanes]
        delta = jnp.sum(
            g.astype(jnp.float32) * o_buf[lines, lanes].astype(jnp.float32), axis=1, keepdims=True
        )

        def scores(b):
            at = b * block_len if isinstance(b, int) else pl.multiple_of(b * block_len, block_len)
            part = pl.ds(at, block_len)
            return part, dot(q, k_buf[part, :], 1, 1) * (scale * LOG2E) + bias[lines, part]

        def terms(part, prob):
            dprob = dot(g, v_buf[part, :], 1, 1)
            dscore = (prob * (dprob - delta) * scale).astype(jnp.bfloat16)
            return prob.astype(jnp.bfloat16), dscore, dot(dscore, k_buf[part, :], 1, 0)

        def pair_terms(part, prob_low, dscore):
            pair_acc[part, :dim] += dot(dscore, q, 0, 0)
            pair_acc[part, dim:] += dot(prob_low, g, 0, 0)

        def start_dq(dq):
            dq_buf[lines, lanes] = dq.astype(jnp.bfloat16)

            @pl.when(sec > 0)
            def _():
                send_dq(h, lines, slot).start()

        if blocks == 1:
            part, score = scores(0)
            top = jnp.max(score, axis=1, keepdims=True)
            prob = jnp.exp2(score - top)
            prob = prob * (1.0 / jnp.sum(prob, axis=1, keepdims=True))
            prob_low, dscore, dq = terms(part, prob)
            start_dq(dq)
            pair_terms(part, prob_low, dscore)
        else:
            stats[0, lines] = jnp.full((lines.size, 1), NEG, jnp.float32)
            stats[1, lines] = jnp.zeros((lines.size, 1), jnp.float32)
            dq_acc[lines] = jnp.zeros((lines.size, dim), jnp.float32)

            def gather_stats(b, _):
                _, score = scores(b)
                before = stats[0, lines]
                top = jnp.maximum(before, jnp.max(score, axis=1, keepdims=True))
                mass = jnp.sum(jnp.exp2(score - top), axis=1, keepdims=True)
                stats[1, lines] = stats[1, lines] * jnp.exp2(before - top) + mass
                stats[0, lines] = top
                return 0

            def gather_terms(b, _):
                part, score = scores(b)
                prob = jnp.exp2(score - stats[0, lines]) * (1.0 / stats[1, lines])
                prob_low, dscore, dq = terms(part, prob)
                dq_acc[lines] += dq
                pair_terms(part, prob_low, dscore)
                return 0

            lax.fori_loop(0, blocks, gather_stats, 0)
            lax.fori_loop(0, blocks, gather_terms, 0)
            start_dq(dq_acc[lines])

    pieces = [(h, pl.ds(0, rows), h) for h in range(heads)]
    for piece in pieces[:1]:
        rows_of_head(*piece)

    @pl.when(sec == sections - 1)
    def _():
        upstream[...] = jnp.zeros_like(upstream)

    for copy in later:
        copy.wait()

    def one_head(h, _):
        rows_of_head(h, pl.ds(0, rows), h)
        return 0

    lax.fori_loop(1, heads, one_head, 0)

    pair_sent = []
    for off in range(1, ranks):
        dst = lax.rem(me + off, ranks)
        pair_sent.append(
            pltpu.make_async_remote_copy(
                src_ref=pair_acc.at[pl.ds(off * rows, rows), :],
                dst_ref=pair_recv.at[off - 1],
                send_sem=pair_send.at[off - 1],
                recv_sem=pair_got.at[off - 1],
                device_id={"cp": dst},
                device_id_type=MESH,
            )
        )
    for copy in pair_sent:
        copy.start()
    for copy in sent:
        copy.wait_send()
    for copy in pair_sent:
        copy.wait_recv()
    total = pair_acc[mine, :]
    for off in range(1, ranks):
        total = total + pair_recv[off - 1]
    key_grad[...] = total[:, :dim].astype(jnp.bfloat16)
    value_grad[...] = total[:, dim:].astype(jnp.bfloat16)
    for copy in pair_sent:
        copy.wait_send()

    @pl.when(sec > 0)
    def _():
        for piece in pieces:
            send_dq(*piece).wait_send()

    @pl.when(sec < sections - 1)
    def _():
        for piece in pieces:
            send_dq(*piece).wait_recv()


def store(key_grad, value_grad, upstream, key_out, value_out, upstream_out, sem):
    copies = [
        pltpu.make_async_copy(src, dst, sem.at[i])
        for i, (src, dst) in enumerate(
            ((upstream, upstream_out), (key_grad, key_out), (value_grad, value_out))
        )
    ]
    for copy in copies:
        copy.start()
    for copy in copies:
        copy.wait()


def body(query, keys, values, attn_out, grad_out, span_pairs):
    _, rows, width = query.shape
    dim = keys.shape[2]
    heads = width // dim
    ranks = lax.axis_size("cp")
    sections = lax.axis_size("pp")
    seq = ranks * rows
    block_len = 2 * rows if ranks % 2 == 0 else rows
    low, full = jnp.bfloat16, jnp.float32
    dma = pltpu.SemaphoreType.DMA
    others = max(ranks - 1, 1)
    vmem = pl.BlockSpec(memory_space=pltpu.VMEM)
    hbm = pl.BlockSpec(memory_space=pltpu.HBM)
    key_grad, value_grad, upstream = pl.pallas_call(
        functools.partial(kernel, ranks, sections, block_len),
        out_shape=(
            pltpu.VMEM((rows, dim), low),
            pltpu.VMEM((rows, dim), low),
            pltpu.VMEM((rows, width), low),
        ),
        in_specs=[pl.BlockSpec(memory_space=pltpu.SMEM)] + [hbm] * 5,
        out_specs=(vmem, vmem, vmem),
        scratch_shapes=[
            pltpu.VMEM((rows, width), low),
            pltpu.VMEM((rows, width), low),
            pltpu.VMEM((rows, width), low),
            pltpu.VMEM((seq, dim), low),
            pltpu.VMEM((seq, dim), low),
            pltpu.VMEM((rows, width), low),
            pltpu.VMEM((rows, seq), full),
            pltpu.VMEM((2, rows, 1), full),
            pltpu.VMEM((rows, dim), full),
            pltpu.VMEM((seq, 2 * dim), full),
            pltpu.VMEM((others, rows, 2 * dim), full),
            dma((8,)),
            dma((2, others)),
            dma((2, others)),
            dma((heads + 1,)),
            dma((heads + 1,)),
            dma((others,)),
            dma((others,)),
        ],
        compiler_params=pltpu.CompilerParams(
            collective_id=0, has_side_effects=True, vmem_limit_bytes=64 * 1024 * 1024 - 1200 * 1024
        ),
        name="backward",
    )(span_pairs, query[0], keys[0], values[0], attn_out[0], grad_out[0])
    anywhere = pl.BlockSpec(memory_space=pl.ANY)
    key_grad, value_grad, upstream = pl.pallas_call(
        store,
        out_shape=(
            jax.ShapeDtypeStruct((rows, dim), low),
            jax.ShapeDtypeStruct((rows, dim), low),
            jax.ShapeDtypeStruct((rows, width), low),
        ),
        in_specs=[anywhere] * 3,
        out_specs=(anywhere,) * 3,
        scratch_shapes=[dma((3,))],
        compiler_params=pltpu.CompilerParams(vmem_limit_bytes=1024 * 1024),
        name="store",
    )(key_grad, value_grad, upstream)
    return key_grad[None], value_grad[None], upstream[None]


def solution(mesh):
    spec = P("pp", "cp", "tp")
    return jax.shard_map(
        body,
        mesh=mesh,
        in_specs=(spec, spec, spec, spec, spec, P()),
        out_specs=(spec, spec, spec),
        check_vma=False,
    )
```

```python
import functools
import math

import jax
import jax.numpy as jnp
from jax import lax
from jax.experimental import pallas as pl
from jax.experimental.pallas import tpu as pltpu
from jax.sharding import PartitionSpec as P

MESH = pl.DeviceIdType.MESH
NEG = -1e30
LOG2E = math.log2(math.e)


def kernel(
    ranks, sections, block_len,
    pairs_hbm, query, keys, values, attn_out, grad_out,
    key_grad, value_grad, upstream,
    q_buf, o_buf, g_buf, k_buf, v_buf, dq_buf, bias, stats, dq_acc, pair_acc, pair_recv,
    pairs, in_sem, kv_send, kv_recv, dq_send, dq_recv, pair_send, pair_got,
):
    rows, width = q_buf.shape
    dim = k_buf.shape[1]
    heads = width // dim
    span = rows // 2
    seq = ranks * rows
    blocks = seq // block_len
    scale = 1.0 / math.sqrt(dim)
    me = lax.axis_index("cp")
    sec = lax.axis_index("pp")
    mine = pl.ds(0, rows)

    barrier = pltpu.get_barrier_semaphore()
    for off in range(1, ranks):
        pl.semaphore_signal(
            barrier, inc=1, device_id={"cp": lax.rem(me + off, ranks)}, device_id_type=MESH
        )

    @pl.when(sec < sections - 1)
    def _():
        pl.semaphore_signal(barrier, inc=1, device_id={"pp": sec + 1}, device_id_type=MESH)

    own = [
        pltpu.make_async_copy(keys, k_buf.at[mine, :], in_sem.at[0]),
        pltpu.make_async_copy(values, v_buf.at[mine, :], in_sem.at[1]),
    ]
    first, rest = pl.ds(0, dim), pl.ds(dim, width - dim)
    wide = ((query, q_buf), (grad_out, g_buf), (attn_out, o_buf))
    begin = [
        pltpu.make_async_copy(src.at[:, first], dst.at[:, first], in_sem.at[2 + i])
        for i, (src, dst) in enumerate(wide)
    ]
    later = [
        pltpu.make_async_copy(src.at[:, rest], dst.at[:, rest], in_sem.at[5 + i])
        for i, (src, dst) in enumerate(wide)
    ]
    table = pltpu.make_async_copy(pairs_hbm, pairs, in_sem.at[8])
    for copy in [table] + own + begin:
        copy.start()

    pl.semaphore_wait(barrier, ranks - 1 + (sec > 0).astype(jnp.int32))
    sent = []
    for off in range(1, ranks):
        for which, (src, buf) in enumerate(((keys, k_buf), (values, v_buf))):
            sent.append(
                pltpu.make_async_remote_copy(
                    src_ref=src,
                    dst_ref=buf.at[pl.ds((ranks - off) * rows, rows), :],
                    send_sem=kv_send.at[which, off - 1],
                    recv_sem=kv_recv.at[which, off - 1],
                    device_id={"cp": lax.rem(me + off, ranks)},
                    device_id_type=MESH,
                )
            )
    for copy in sent + later:
        copy.start()

    table.wait()
    row = lax.broadcasted_iota(jnp.int32, (rows, rows), 0)
    col = lax.broadcasted_iota(jnp.int32, (rows, rows), 1)
    q_pos = jnp.where(row < span, pairs[me, 0] * span, pairs[me, 1] * span - span) + row
    for r in range(ranks):
        rank = lax.rem(me + r, ranks)
        k_pos = jnp.where(col < span, pairs[rank, 0] * span, pairs[rank, 1] * span - span) + col
        bias[:, r * rows:(r + 1) * rows] = jnp.where(k_pos <= q_pos, 0.0, NEG)
    pair_acc[...] = jnp.zeros_like(pair_acc)

    for copy in own + begin:
        copy.wait()
    for copy in sent:
        copy.wait_recv()

    def dot(a, b, da, db):
        return lax.dot_general(a, b, (((da,), (db,)), ((), ())), preferred_element_type=jnp.float32)

    def lanes_of(h):
        return pl.ds(h * dim if isinstance(h, int) else pl.multiple_of(h * dim, dim), dim)

    def send_dq(h, lines, slot):
        return pltpu.make_async_remote_copy(
            src_ref=dq_buf.at[lines, lanes_of(h)],
            dst_ref=upstream.at[lines, lanes_of(h)],
            send_sem=dq_send.at[slot],
            recv_sem=dq_recv.at[slot],
            device_id={"pp": jnp.maximum(sec - 1, 0)},
            device_id_type=MESH,
        )

    def rows_of_head(h, lines, slot):
        lanes = lanes_of(h)
        q = q_buf[lines, lanes]
        g = g_buf[lines, lanes]
        delta = jnp.sum(
            g.astype(jnp.float32) * o_buf[lines, lanes].astype(jnp.float32), axis=1, keepdims=True
        )

        def scores(b):
            at = b * block_len if isinstance(b, int) else pl.multiple_of(b * block_len, block_len)
            part = pl.ds(at, block_len)
            return part, dot(q, k_buf[part, :], 1, 1) * (scale * LOG2E) + bias[lines, part]

        def terms(part, prob):
            dprob = dot(g, v_buf[part, :], 1, 1)
            dscore = (prob * (dprob - delta) * scale).astype(jnp.bfloat16)
            return prob.astype(jnp.bfloat16), dscore, dot(dscore, k_buf[part, :], 1, 0)

        def pair_terms(part, prob_low, dscore):
            pair_acc[part, :dim] += dot(dscore, q, 0, 0)
            pair_acc[part, dim:] += dot(prob_low, g, 0, 0)

        def start_dq(dq):
            dq_buf[lines, lanes] = dq.astype(jnp.bfloat16)

            @pl.when(sec > 0)
            def _():
                send_dq(h, lines, slot).start()

        if blocks == 1:
            part, score = scores(0)
            top = jnp.max(score, axis=1, keepdims=True)
            prob = jnp.exp2(score - top)
            prob = prob * (1.0 / jnp.sum(prob, axis=1, keepdims=True))
            prob_low, dscore, dq = terms(part, prob)
            start_dq(dq)
            pair_terms(part, prob_low, dscore)
        else:
            stats[0, lines] = jnp.full((lines.size, 1), NEG, jnp.float32)
            stats[1, lines] = jnp.zeros((lines.size, 1), jnp.float32)
            dq_acc[lines] = jnp.zeros((lines.size, dim), jnp.float32)

            def gather_stats(b, _):
                _, score = scores(b)
                before = stats[0, lines]
                top = jnp.maximum(before, jnp.max(score, axis=1, keepdims=True))
                mass = jnp.sum(jnp.exp2(score - top), axis=1, keepdims=True)
                stats[1, lines] = stats[1, lines] * jnp.exp2(before - top) + mass
                stats[0, lines] = top
                return 0

            def gather_terms(b, _):
                part, score = scores(b)
                prob = jnp.exp2(score - stats[0, lines]) * (1.0 / stats[1, lines])
                prob_low, dscore, dq = terms(part, prob)
                dq_acc[lines] += dq
                pair_terms(part, prob_low, dscore)
                return 0

            lax.fori_loop(0, blocks, gather_stats, 0)
            lax.fori_loop(0, blocks, gather_terms, 0)
            start_dq(dq_acc[lines])

    pieces = [(h, pl.ds(0, rows), h) for h in range(heads)]
    for piece in pieces[:1]:
        rows_of_head(*piece)

    @pl.when(sec == sections - 1)
    def _():
        upstream[...] = jnp.zeros_like(upstream)

    for copy in later:
        copy.wait()

    def one_head(h, _):
        rows_of_head(h, pl.ds(0, rows), h)
        return 0

    lax.fori_loop(1, heads, one_head, 0)

    pair_sent = []
    for off in range(1, ranks):
        dst = lax.rem(me + off, ranks)
        pair_sent.append(
            pltpu.make_async_remote_copy(
                src_ref=pair_acc.at[pl.ds(off * rows, rows), :],
                dst_ref=pair_recv.at[off - 1],
                send_sem=pair_send.at[off - 1],
                recv_sem=pair_got.at[off - 1],
                device_id={"cp": dst},
                device_id_type=MESH,
            )
        )
    for copy in pair_sent:
        copy.start()
    for copy in sent:
        copy.wait_send()
    for copy in pair_sent:
        copy.wait_recv()
    total = pair_acc[mine, :]
    for off in range(1, ranks):
        total = total + pair_recv[off - 1]
    key_grad[...] = total[:, :dim].astype(jnp.bfloat16)
    value_grad[...] = total[:, dim:].astype(jnp.bfloat16)
    for copy in pair_sent:
        copy.wait_send()

    @pl.when(sec > 0)
    def _():
        for piece in pieces:
            send_dq(*piece).wait_send()

    @pl.when(sec < sections - 1)
    def _():
        for piece in pieces:
            send_dq(*piece).wait_recv()


def store(key_grad, value_grad, upstream, key_out, value_out, upstream_out, sem):
    copies = [
        pltpu.make_async_copy(src, dst, sem.at[i])
        for i, (src, dst) in enumerate(
            ((upstream, upstream_out), (key_grad, key_out), (value_grad, value_out))
        )
    ]
    for copy in copies:
        copy.start()
    for copy in copies:
        copy.wait()


def body(query, keys, values, attn_out, grad_out, span_pairs):
    _, rows, width = query.shape
    dim = keys.shape[2]
    heads = width // dim
    ranks = lax.axis_size("cp")
    sections = lax.axis_size("pp")
    seq = ranks * rows
    block_len = 2 * rows if ranks % 2 == 0 else rows
    low, full = jnp.bfloat16, jnp.float32
    dma = pltpu.SemaphoreType.DMA
    others = max(ranks - 1, 1)
    vmem = pl.BlockSpec(memory_space=pltpu.VMEM)
    hbm = pl.BlockSpec(memory_space=pltpu.HBM)
    key_grad, value_grad, upstream = pl.pallas_call(
        functools.partial(kernel, ranks, sections, block_len),
        out_shape=(
            pltpu.VMEM((rows, dim), low),
            pltpu.VMEM((rows, dim), low),
            pltpu.VMEM((rows, width), low),
        ),
        in_specs=[hbm] * 6,
        out_specs=(vmem, vmem, vmem),
        scratch_shapes=[
            pltpu.VMEM((rows, width), low),
            pltpu.VMEM((rows, width), low),
            pltpu.VMEM((rows, width), low),
            pltpu.VMEM((seq, dim), low),
            pltpu.VMEM((seq, dim), low),
            pltpu.VMEM((rows, width), low),
            pltpu.VMEM((rows, seq), full),
            pltpu.VMEM((2, rows, 1), full),
            pltpu.VMEM((rows, dim), full),
            pltpu.VMEM((seq, 2 * dim), full),
            pltpu.VMEM((others, rows, 2 * dim), full),
            pltpu.SMEM((ranks, 2), jnp.int32),
            dma((9,)),
            dma((2, others)),
            dma((2, others)),
            dma((heads + 1,)),
            dma((heads + 1,)),
            dma((others,)),
            dma((others,)),
        ],
        compiler_params=pltpu.CompilerParams(
            collective_id=0, has_side_effects=True, vmem_limit_bytes=64 * 1024 * 1024 - 1200 * 1024
        ),
        name="backward",
    )(span_pairs, query[0], keys[0], values[0], attn_out[0], grad_out[0])
    anywhere = pl.BlockSpec(memory_space=pl.ANY)
    key_grad, value_grad, upstream = pl.pallas_call(
        store,
        out_shape=(
            jax.ShapeDtypeStruct((rows, dim), low),
            jax.ShapeDtypeStruct((rows, dim), low),
            jax.ShapeDtypeStruct((rows, width), low),
        ),
        in_specs=[anywhere] * 3,
        out_specs=(anywhere,) * 3,
        scratch_shapes=[dma((3,))],
        compiler_params=pltpu.CompilerParams(vmem_limit_bytes=1024 * 1024),
        name="store",
    )(key_grad, value_grad, upstream)
    return key_grad[None], value_grad[None], upstream[None]


def solution(mesh):
    spec = P("pp", "cp", "tp")
    return jax.shard_map(
        body,
        mesh=mesh,
        in_specs=(spec, spec, spec, spec, spec, P()),
        out_specs=(spec, spec, spec),
        check_vma=False,
    )
```
